32 devices in a mesh: dp: 4 (over y, core), fsdp: 8 (over z, x).
Axes of the slice: x: 2, y: 2, z: 4, core: 2. Of those that a mesh axis runs over, the one named last changes fastest.
Arguments:
- tokens: bfloat16 [4096, 1536], P(('dp', 'fsdp')), may hold values from -6 to 6
- seq_ids: int32 [32, 128], P(('dp', 'fsdp')), may hold values from 0 to 127, as said below
- routes: int32 [4096, 8], P(('dp', 'fsdp')), may hold values from 0 to 39, all different within a row; in each aligned block of 128 rows (0 to 127, 128 to 255, ...) at most 32 rows name the same one
- cotangent: bfloat16 [4096, 1536], P(('dp', 'fsdp')), may hold values from -6 to 6
- gain_attn: bfloat16 [1536], P(('dp', 'fsdp')), may hold values from 0.5 to 1.5
- qkv_weight: bfloat16 [1536, 2560], P(('dp', 'fsdp')), may hold values from -0.15625 to 0.15625
- out_weight: bfloat16 [1536, 1536], P(('dp', 'fsdp')), may hold values from -0.625 to 0.625
- gain_moe: bfloat16 [1536], P(('dp', 'fsdp')), may hold values from 0.5 to 1.5
- router_weight: bfloat16 [1536, 40], P(('dp', 'fsdp')), may hold values from -0.3125 to 0.3125
- expert_weight: bfloat16 [40, 1536, 1536], P('dp', 'fsdp'), may hold values from -0.3125 to 0.3125
Outputs:
- block_out: bfloat16 [4096, 1536], P(('dp', 'fsdp'))
- d_tokens: float32 [4096, 1536], P(('dp', 'fsdp'))
- d_gain_attn: float32 [1536], P(('dp', 'fsdp'))
- d_qkv_weight: float32 [1536, 2560], P(('dp', 'fsdp'))
- d_out_weight: float32 [1536, 1536], P(('dp', 'fsdp'))
- d_gain_moe: float32 [1536], P(('dp', 'fsdp'))
- d_router_weight: float32 [1536, 40], P(('dp', 'fsdp'))
- d_expert_weight: float32 [40, 1536, 1536], P('dp', 'fsdp')
The draws below stay inside these ranges and needn't reach their ends.
Inputs may be any that keep to these rules, and one draw needn't show every extreme that they name: `routes`: in each device's 128 rows no expert is named more than 32 times, a bound that some block reaches. `seq_ids`: within each row the ids start at 0 and rise by 0 or 1 from slot to slot; every sequence has 1 to 128 tokens; some row holds a single sequence of 128 tokens, and some row holds 128 sequences of one token.
All inputs are finite; a program needn't handle non-finite values.
Results may differ from the reference program's by a relative error of at most 0.018.
Values may be sent and summed in bfloat16 or wider, within the bound.
No kernel may reach another device: no remote copies, remote signals or barrier semaphores. Data moves between devices by JAX's collectives and lax.ppermute only.
A program may use at most 384 MiB of HBM per device.

```python
import math
import jax
import jax.numpy as jnp
import numpy as np
from jax import lax

D = 1536
H = 24
KV = 8
HD = 64
F = 512
E = 40
TOPK = 8
TOK_DEV = 128
CAP = 32
TOKENS = 4096
N_DP = 4
N_FSDP = 8


def draw_seq_ids(key, part):
    devices = N_DP * N_FSDP
    first_key, second_key, third_key = jax.random.split(jax.random.fold_in(key, 7), 3)
    starts = jnp.where(jax.random.randint(first_key, (devices, TOK_DEV), 0, 48) == 0, 1, 0).astype(jnp.int32)
    offset = jax.random.randint(second_key, (), 0, 8)
    whole_rows = ((jnp.arange(devices) + offset) % 8 == 0)[:, None]
    starts = jnp.where(whole_rows, 0, starts)
    single_row = 8 * jax.random.randint(third_key, (), 0, devices // 8) + (4 - offset) % 8
    starts = jnp.where((jnp.arange(devices) == single_row)[:, None], 1, starts)
    starts = starts.at[:, 0].set(0)
    return jnp.cumsum(starts, axis=1).astype(jnp.int32)


def block_scale(stream_key, dims, pieces, smallest, top_value):
    def one(dim, shards_of):
        steps = jax.random.uniform(jax.random.fold_in(jax.random.fold_in(stream_key, 6), dim), (shards_of,), jnp.float32, smallest / len(pieces), top_value / len(pieces))
        return jnp.repeat(jnp.exp(steps), dims[dim] // shards_of).reshape((-1,) + (1,) * (len(dims) - dim - 1))

    factor_of = one(*pieces[0])
    for cut in pieces[1:]:
        factor_of = factor_of * one(*cut)
    return factor_of


def shared_out(key, own, number, rows, count, top, limit, slope):
    order = jax.random.permutation(key, count)
    packed, ordinary = shares(count, rows * top, limit, slope, True), shares(count, rows * top, limit, slope, False)
    places = jnp.arange(count)

    def named(lengths, rotation):
        used = int((lengths > 0).sum())
        fixed = max(1, used // 4)
        moved = fixed + (places - fixed + rotation * (used - fixed)) % max(1, count - fixed)
        return jnp.zeros((count,), jnp.int32).at[order[jnp.where(places < fixed, places, moved)]].set(jnp.asarray(lengths, jnp.int32))

    lengths = jnp.where(number % 4 == 0, named(packed, number // 4), named(ordinary, number - number // 4 - 1))
    mixed = jax.random.permutation(jax.random.fold_in(own, 3), count)
    source_of, sink = mixed[0:count // 2 * 2:2], mixed[1:count // 2 * 2:2]
    margin = jnp.minimum(lengths[source_of] - 1, limit - lengths[sink]) // 2
    margin = jnp.where((source_of == order[0]) | (sink == order[0]) | (lengths[sink] == 0), 0, jnp.maximum(margin, 0))
    moved = jax.random.randint(jax.random.fold_in(own, 4), (count // 2,), 0, 1 << 20) % (margin + 1)
    lengths = lengths.at[source_of].add(-moved).at[sink].add(moved)
    labels = jnp.searchsorted(jnp.cumsum(lengths), jnp.arange(rows * top), side="right").astype(jnp.int32)
    table = labels.reshape(top, rows).T
    table = table[jax.random.permutation(jax.random.fold_in(own, 1), rows)]
    rotation = jax.random.randint(jax.random.fold_in(own, 2), (rows, 1), 0, top)
    return jnp.take_along_axis(table, (jnp.arange(top)[None, :] + rotation) % top, axis=1)


def shares(number_of, total, reach, lean, full):
    loads = [(1 << 20) // math.isqrt(grade ** lean) + 1 for grade in range(1, number_of + 1)]
    largest = reach if full else min(reach, max(-(-total // number_of), total * loads[0] // sum(loads)))
    least = 1 if total - largest >= number_of - 1 else 0
    given, rest = [largest] + [least] * (number_of - 1), total - largest - least * (number_of - 1)
    while rest > 0:
        movable = [i for i in range(1, number_of) if given[i] < largest] or [i for i in range(1, number_of) if given[i] < reach]
        whole, budget = sum([loads[i] for i in movable]), rest
        for i in movable:
            extra = min(reach - given[i], max(1, budget * loads[i] // whole), rest)
            given[i] = given[i] + extra
            rest = rest - extra
    return np.array(given)


def gaussian(key, extent, deviation, reach, cuts=(), kind=jnp.bfloat16):
    result = jax.random.normal(key, extent, jnp.float32) * deviation
    if len(cuts) > 0:
        result = block_scale(key, extent, cuts, -0.22, 0.18) * result
    return jnp.clip(result, min=-reach, max=reach).astype(kind)


def setup_inputs(seed: int = 0) -> dict:
    keys = jax.random.split(jax.random.key(seed), 11)
    tokens = gaussian(keys[0], (TOKENS, D), 1.0, 6.0, ((0, 32),))
    seq_ids = draw_seq_ids(jax.random.fold_in(keys[10], 71), 0)
    routes_keys = jax.random.split(jax.random.fold_in(keys[2], 1), TOKENS // TOK_DEV)
    routes_turns = jax.random.permutation(jax.random.fold_in(keys[2], 3), TOKENS // TOK_DEV)
    routes = jax.vmap(lambda own, number: shared_out(jax.random.fold_in(keys[2], 2), own, number, TOK_DEV, E, TOPK, CAP, 1))(routes_keys, routes_turns).reshape((TOKENS, TOPK))
    cotangent = gaussian(keys[3], (TOKENS, D), 1.0, 6.0, ((0, 32),))
    gain_attn = jnp.clip(1.0 + 0.1 * jax.random.normal(keys[4], (D,), jnp.float32), 0.5, 1.5).astype(jnp.bfloat16)
    qkv_weight = gaussian(keys[5], (D, (H + 2 * KV) * HD), D ** -0.5, 0.15625, ((0, 32),))
    out_weight = gaussian(keys[6], (H * HD, D), (D // 16) ** -0.5, 0.625, ((0, 32),))
    gain_moe = jnp.clip(1.0 + 0.1 * jax.random.normal(keys[7], (D,), jnp.float32), 0.5, 1.5).astype(jnp.bfloat16)
    router_weight = gaussian(keys[8], (D, E), (D // 4) ** -0.5, 0.3125, ((0, 32),))
    expert_weight = gaussian(keys[9], (E, D, 3 * F), (D // 4) ** -0.5, 0.3125, ((0, 4), (1, 8)))
    return dict(tokens=tokens, seq_ids=seq_ids, routes=routes, cotangent=cotangent, gain_attn=gain_attn, qkv_weight=qkv_weight, out_weight=out_weight, gain_moe=gain_moe, router_weight=router_weight, expert_weight=expert_weight)


norm_eps = 1e-06

def rounded(values):
    return lax.optimization_barrier(values.astype(jnp.bfloat16)).astype(jnp.float32)

def rope_tables(seq_row, half_width):
    length = seq_row.shape[0]
    places = jnp.arange(length)
    same_seq = seq_row[:, None] == seq_row[None, :]
    earlier = places[None, :] < places[:, None]
    position = lax.optimization_barrier(jnp.sum(jnp.where(same_seq & earlier, 1, 0), axis=1)).astype(jnp.int32)
    inverse = 10000.0 ** (-jnp.arange(half_width).astype(jnp.float32) / half_width)
    angles = position.astype(jnp.float32)[:, None] * inverse[None, :]
    visible = same_seq & (places[None, :] <= places[:, None])
    return (jnp.cos(angles), jnp.sin(angles), visible)

def rotate(values, cosine, sine_table):
    half_width = values.shape[-1] // 2
    first_half = values[..., :half_width]
    second_half = values[..., half_width:]
    cos_wide = cosine[:, None, :]
    sin_wide = sine_table[:, None, :]
    return jnp.concatenate([first_half * cos_wide - second_half * sin_wide, second_half * cos_wide + first_half * sin_wide], axis=-1)

def unrotate(grad_rows, cosine, sine_table):
    half_width = grad_rows.shape[-1] // 2
    first_half = grad_rows[..., :half_width]
    second_half = grad_rows[..., half_width:]
    cos_wide = cosine[:, None, :]
    sin_wide = sine_table[:, None, :]
    return jnp.concatenate([first_half * cos_wide + second_half * sin_wide, second_half * cos_wide - first_half * sin_wide], axis=-1)

def norm_forward(values, gain_vec):
    inv_rms = lax.rsqrt(lax.optimization_barrier(jnp.mean(values * values, axis=-1, keepdims=True)) + norm_eps)
    return (inv_rms, values * inv_rms * gain_vec.astype(jnp.float32))

def norm_backward(values, inv_rms, gain_vec, upstream):
    weighted = upstream * gain_vec.astype(jnp.float32)
    d_gain = lax.optimization_barrier(jnp.sum(upstream * values * inv_rms, axis=0))
    d_values = inv_rms * (weighted - values * inv_rms * inv_rms * lax.optimization_barrier(jnp.mean(weighted * values, axis=-1, keepdims=True)))
    return (d_values, d_gain)

def attend_group(group_in, visible, factor):
    queries, keys_rot, values_in = group_in
    scores = jnp.einsum('gqd,kd->gqk', queries.astype(jnp.float32), keys_rot.astype(jnp.float32)) * factor
    exp_scores = jnp.where(visible[None], jnp.exp(scores), 0.0)
    totals = lax.optimization_barrier(jnp.sum(exp_scores, axis=-1))
    attn_probs = (exp_scores / totals[..., None]).astype(jnp.bfloat16)
    mixed_heads = jnp.einsum('gqk,kd->gqd', attn_probs.astype(jnp.float32), values_in.astype(jnp.float32))
    return (mixed_heads.astype(jnp.bfloat16), jnp.log(totals))

def attend_back(group_in, visible, factor):
    queries, keys_rot, values_in, mixed_heads, log_totals, d_mixed = group_in
    query_wide = queries.astype(jnp.float32)
    keys_wide = keys_rot.astype(jnp.float32)
    values_wide = values_in.astype(jnp.float32)
    d_mixed_wide = d_mixed.astype(jnp.float32)
    scores = jnp.einsum('gqd,kd->gqk', query_wide, keys_wide) * factor
    recomputed = jnp.where(visible[None], jnp.exp(scores - log_totals[..., None]), 0.0)
    row_delta = lax.optimization_barrier(jnp.sum(d_mixed_wide * mixed_heads.astype(jnp.float32), axis=-1))
    d_probs = jnp.einsum('gqd,kd->gqk', d_mixed_wide, values_wide)
    d_scores = rounded(recomputed * (d_probs - row_delta[..., None]))
    d_query = jnp.einsum('gqk,kd->gqd', d_scores, keys_wide) * factor
    d_keys = jnp.einsum('gqk,gqd->kd', d_scores, query_wide) * factor
    d_values = jnp.einsum('gqk,gqd->kd', rounded(recomputed), d_mixed_wide)
    return (d_query, d_keys, d_values)

def dispatch_plan(route_row, experts, capacity):
    flat_routes = route_row.reshape(-1)
    pair_count = flat_routes.shape[0]
    hit_table = (flat_routes[:, None] == jnp.arange(experts)[None, :]).astype(jnp.int32)
    earlier = jnp.cumsum(hit_table, axis=0) - hit_table
    slot_index = lax.optimization_barrier(jnp.sum(earlier * hit_table, axis=1))
    places = (flat_routes * capacity + slot_index).astype(jnp.int32)
    source = jnp.full((experts * capacity,), pair_count, jnp.int32).at[places].set(jnp.arange(pair_count).astype(jnp.int32))
    return (places, source)

def expert_forward(slot_rows, weight):
    hidden_width = weight.shape[-1] // 3
    up_proj = weight[..., :2 * hidden_width].astype(jnp.float32)
    down_proj = weight[..., 2 * hidden_width:].astype(jnp.float32)
    both_parts = jnp.einsum('ecd,edf->ecf', slot_rows.astype(jnp.float32), up_proj)
    gate_part = both_parts[..., :hidden_width]
    up_part = both_parts[..., hidden_width:]
    hidden = rounded(gate_part * jax.nn.sigmoid(gate_part) * up_part)
    return jnp.einsum('ecf,edf->ecd', hidden, down_proj).astype(jnp.bfloat16)

def expert_backward(slot_rows, d_slots, weight):
    hidden_width = weight.shape[-1] // 3
    rows_wide = slot_rows.astype(jnp.float32)
    d_slots_wide = d_slots.astype(jnp.float32)
    up_proj = weight[..., :2 * hidden_width].astype(jnp.float32)
    down_proj = weight[..., 2 * hidden_width:].astype(jnp.float32)
    both_parts = jnp.einsum('ecd,edf->ecf', rows_wide, up_proj)
    gate_part = both_parts[..., :hidden_width]
    up_part = both_parts[..., hidden_width:]
    sigmoid_gate = jax.nn.sigmoid(gate_part)
    hidden = rounded(gate_part * sigmoid_gate * up_part)
    d_hidden = jnp.einsum('ecd,edf->ecf', d_slots_wide, down_proj)
    d_both = rounded(jnp.concatenate([d_hidden * up_part * sigmoid_gate * (1.0 + gate_part * (1.0 - sigmoid_gate)), d_hidden * gate_part * sigmoid_gate], axis=-1))
    d_input = jnp.einsum('ecf,edf->ecd', d_both, up_proj).astype(jnp.bfloat16)
    grad_term = jnp.concatenate([jnp.einsum('ecd,ecf->edf', rows_wide, d_both), jnp.einsum('ecd,ecf->edf', d_slots_wide, hidden)], axis=-1)
    return (d_input, grad_term)

def layer_pass(weights_all, tokens, seq_row, route_row, cotangent):
    gain_attn, qkv_weight, out_weight, gain_moe, router_weight, expert_weight = weights_all
    length = tokens.shape[0]
    top_count = route_row.shape[1]
    query_width = H * HD
    kv_width = KV * HD
    group_size = H // KV
    factor = HD ** (-0.5)
    cosine, sine_table, visible = rope_tables(seq_row, HD // 2)
    stream_in = tokens.astype(jnp.float32)
    inv_one, normed = norm_forward(stream_in, gain_attn)
    normed_one = normed.astype(jnp.bfloat16)
    qkv_proj = jnp.dot(normed_one, qkv_weight, preferred_element_type=jnp.float32)
    queries = rotate(qkv_proj[:, :query_width].reshape(length, H, HD), cosine, sine_table).astype(jnp.bfloat16)
    keys_rot = rotate(qkv_proj[:, query_width:query_width + kv_width].reshape(length, KV, HD), cosine, sine_table).astype(jnp.bfloat16)
    values_in = qkv_proj[:, query_width + kv_width:].reshape(length, KV, HD).astype(jnp.bfloat16)
    query_groups = queries.reshape(length, KV, group_size, HD).transpose(1, 2, 0, 3)
    key_groups = keys_rot.transpose(1, 0, 2)
    value_groups = values_in.transpose(1, 0, 2)

    def forward_group(group_in):
        return attend_group(group_in, visible, factor)
    mixed_groups, log_totals = lax.map(forward_group, (query_groups, key_groups, value_groups))
    mixed_flat = mixed_groups.transpose(2, 0, 1, 3).reshape(length, query_width)
    resid_mid = stream_in + jnp.dot(mixed_flat, out_weight, preferred_element_type=jnp.float32)
    inv_two, normed = norm_forward(resid_mid, gain_moe)
    normed_two = normed.astype(jnp.bfloat16)
    logits = jnp.dot(normed_two, router_weight, preferred_element_type=jnp.float32)
    chosen = route_row[:, :, None] == jnp.arange(E)[None, None, :]
    picked = lax.optimization_barrier(jnp.sum(jnp.where(chosen, logits[:, None, :], 0.0), axis=-1))
    exp_picked = jnp.exp(picked)
    gate_probs = exp_picked / lax.optimization_barrier(jnp.sum(exp_picked, axis=-1, keepdims=True))
    places, source = dispatch_plan(route_row, E, CAP)
    token_of = source // top_count
    padded_rows = jnp.concatenate([normed_two, jnp.zeros((1, D), jnp.bfloat16)], axis=0)
    slot_rows = padded_rows[token_of].reshape(E, CAP, D)
    expert_result = expert_forward(slot_rows, expert_weight)
    gathered = expert_result.reshape(E * CAP, D)[places].reshape(length, top_count, D).astype(jnp.float32)
    expert_sum = lax.optimization_barrier(jnp.sum(gate_probs[:, :, None] * gathered, axis=1))
    block_out = (resid_mid + expert_sum).astype(jnp.bfloat16)
    d_block = cotangent.astype(jnp.float32)
    d_gates = lax.optimization_barrier(jnp.sum(gathered * d_block[:, None, :], axis=-1))
    d_picked = gate_probs * (d_gates - lax.optimization_barrier(jnp.sum(gate_probs * d_gates, axis=-1, keepdims=True)))
    d_logits = lax.optimization_barrier(jnp.sum(jnp.where(chosen, d_picked[:, :, None], 0.0), axis=1)).astype(jnp.bfloat16)
    gate_padded = jnp.concatenate([gate_probs.reshape(-1), jnp.zeros((1,), jnp.float32)])
    block_padded = jnp.concatenate([d_block, jnp.zeros((1, D), jnp.float32)], axis=0)
    d_slots = (gate_padded[source][:, None] * block_padded[token_of]).astype(jnp.bfloat16).reshape(E, CAP, D)
    d_expert_in, d_expert = expert_backward(slot_rows, d_slots, expert_weight)
    d_normed_two = lax.optimization_barrier(jnp.sum(d_expert_in.reshape(E * CAP, D)[places].reshape(length, top_count, D).astype(jnp.float32), axis=1))
    d_normed_two = d_normed_two + jnp.dot(d_logits, router_weight.T, preferred_element_type=jnp.float32)
    d_router = jnp.dot(normed_two.T, d_logits, preferred_element_type=jnp.float32)
    d_resid, d_gain_two = norm_backward(resid_mid, inv_two, gain_moe, d_normed_two)
    d_resid = d_resid + d_block
    d_resid_half = d_resid.astype(jnp.bfloat16)
    d_out = jnp.dot(mixed_flat.T, d_resid_half, preferred_element_type=jnp.float32)
    d_mixed = jnp.dot(d_resid_half, out_weight.T, preferred_element_type=jnp.float32).astype(jnp.bfloat16)
    d_mixed_groups = d_mixed.reshape(length, KV, group_size, HD).transpose(1, 2, 0, 3)

    def backward_group(group_in):
        return attend_back(group_in, visible, factor)
    d_query, d_keys, d_values = lax.map(backward_group, (query_groups, key_groups, value_groups, mixed_groups, log_totals, d_mixed_groups))
    d_query = unrotate(d_query.transpose(2, 0, 1, 3).reshape(length, H, HD), cosine, sine_table)
    d_keys = unrotate(d_keys.transpose(1, 0, 2), cosine, sine_table)
    d_qkv_act = jnp.concatenate([d_query.reshape(length, query_width), d_keys.reshape(length, kv_width), d_values.transpose(1, 0, 2).reshape(length, kv_width)], axis=-1).astype(jnp.bfloat16)
    d_qkv = jnp.dot(normed_one.T, d_qkv_act, preferred_element_type=jnp.float32)
    d_normed_one = jnp.dot(d_qkv_act, qkv_weight.T, preferred_element_type=jnp.float32)
    d_stream, d_gain_one = norm_backward(stream_in, inv_one, gain_attn, d_normed_one)
    d_tokens = d_stream + d_resid
    return (block_out, d_tokens, (d_gain_one, d_qkv, d_out, d_gain_two, d_router, d_expert))

def reference(tokens, seq_ids, routes, cotangent, gain_attn, qkv_weight, out_weight, gain_moe, router_weight, expert_weight):
    devices = N_DP * N_FSDP
    weights_all = (gain_attn, qkv_weight, out_weight, gain_moe, router_weight, expert_weight)
    inputs = (tokens.reshape(devices, TOK_DEV, D), seq_ids, routes.reshape(devices, TOK_DEV, TOPK), cotangent.reshape(devices, TOK_DEV, D))
    initial = tuple((jnp.zeros(weight.shape, jnp.float32) for weight in weights_all))

    def device_step(carried, device_in):
        block_out, d_tokens, grad_parts = layer_pass(weights_all, device_in[0], device_in[1], device_in[2], device_in[3])
        summed = tuple((left + right for left, right in zip(carried, grad_parts)))
        return (summed, (block_out, d_tokens))
    totals, (outputs, d_inputs) = lax.scan(device_step, initial, inputs)
    return (outputs.reshape(devices * TOK_DEV, D), d_inputs.reshape(devices * TOK_DEV, D), totals[0], totals[1], totals[2], totals[3], totals[4], totals[5])
```

```python
import functools
import math

import jax
import jax.numpy as jnp
import numpy as np
from jax import lax
from jax.experimental import pallas as pl
from jax.experimental.pallas import tpu as pltpu
from jax.sharding import PartitionSpec as P

D = 1536
H = 24
KV = 8
HD = 64
E = 40
CAP = 32
AXES = ("dp", "fsdp")


norm_eps = 1e-06


def rope_tables(seq_row, half_width):
    length = seq_row.shape[0]
    places = jnp.arange(length)
    same_seq = seq_row[:, None] == seq_row[None, :]
    earlier = places[None, :] < places[:, None]
    position = jnp.sum(jnp.where(same_seq & earlier, 1, 0), axis=1).astype(jnp.int32)
    inverse = 10000.0 ** (-jnp.arange(half_width).astype(jnp.float32) / half_width)
    angles = position.astype(jnp.float32)[:, None] * inverse[None, :]
    visible = same_seq & (places[None, :] <= places[:, None])
    return (jnp.cos(angles), jnp.sin(angles), visible)


def rotate(values, cosine, sine_table):
    half_width = values.shape[-1] // 2
    first_half = values[..., :half_width]
    second_half = values[..., half_width:]
    cos_wide = cosine[:, None, :]
    sin_wide = sine_table[:, None, :]
    return jnp.concatenate(
        [
            first_half * cos_wide - second_half * sin_wide,
            second_half * cos_wide + first_half * sin_wide,
        ],
        axis=-1,
    )


def unrotate(grad_rows, cosine, sine_table):
    half_width = grad_rows.shape[-1] // 2
    first_half = grad_rows[..., :half_width]
    second_half = grad_rows[..., half_width:]
    cos_wide = cosine[:, None, :]
    sin_wide = sine_table[:, None, :]
    return jnp.concatenate(
        [
            first_half * cos_wide + second_half * sin_wide,
            second_half * cos_wide - first_half * sin_wide,
        ],
        axis=-1,
    )


def norm_forward(values, gain_vec):
    inv_rms = lax.rsqrt(jnp.mean(values * values, axis=-1, keepdims=True) + norm_eps)
    return (inv_rms, values * inv_rms * gain_vec.astype(jnp.float32))


def norm_backward(values, inv_rms, gain_vec, upstream):
    weighted = upstream * gain_vec.astype(jnp.float32)
    d_gain = jnp.sum(upstream * values * inv_rms, axis=0)
    d_values = inv_rms * (
        weighted - values * inv_rms * inv_rms * jnp.mean(weighted * values, axis=-1, keepdims=True)
    )
    return (d_values, d_gain)


def attend_group(group_in, visible, factor):
    queries, keys_rot, values_in = group_in
    scores = (
        jnp.einsum("gqd,kd->gqk", queries, keys_rot, preferred_element_type=jnp.float32) * factor
    )
    exp_scores = jnp.where(visible[None], jnp.exp(scores), 0.0)
    totals = jnp.sum(exp_scores, axis=-1)
    attn_probs = (exp_scores / totals[..., None]).astype(jnp.bfloat16)
    mixed_heads = jnp.einsum(
        "gqk,kd->gqd", attn_probs, values_in, preferred_element_type=jnp.float32
    )
    return (mixed_heads.astype(jnp.bfloat16), jnp.log(totals))


def attend_back(group_in, visible, factor):
    queries, keys_rot, values_in, mixed_heads, log_totals, d_mixed = group_in
    scores = (
        jnp.einsum("gqd,kd->gqk", queries, keys_rot, preferred_element_type=jnp.float32) * factor
    )
    recomputed = jnp.where(visible[None], jnp.exp(scores - log_totals[..., None]), 0.0)
    row_delta = jnp.sum(d_mixed.astype(jnp.float32) * mixed_heads.astype(jnp.float32), axis=-1)
    d_probs = jnp.einsum("gqd,kd->gqk", d_mixed, values_in, preferred_element_type=jnp.float32)
    d_scores = (recomputed * (d_probs - row_delta[..., None])).astype(jnp.bfloat16)
    d_query = (
        jnp.einsum("gqk,kd->gqd", d_scores, keys_rot, preferred_element_type=jnp.float32) * factor
    )
    d_keys = (
        jnp.einsum("gqk,gqd->kd", d_scores, queries, preferred_element_type=jnp.float32) * factor
    )
    d_values = jnp.einsum(
        "gqk,gqd->kd", recomputed.astype(jnp.bfloat16), d_mixed, preferred_element_type=jnp.float32
    )
    return (d_query, d_keys, d_values)


def bit_groups():
    dp_count, fsdp_count = lax.axis_size("dp"), lax.axis_size("fsdp")
    fsdp_bits = int(math.log2(fsdp_count))
    low = fsdp_bits // 2
    near = [m for m in range(1, 1 << low)]
    far = [m << low for m in range(1, fsdp_count >> low)]
    core = fsdp_count
    rows = [m * 2 * fsdp_count for m in range(1, dp_count // 2)]
    return far, near, rows, core


def swap(value, mask):
    count = lax.axis_size("dp") * lax.axis_size("fsdp")
    return lax.ppermute(value, AXES, [(i, i ^ mask) for i in range(count)])


def mask_order():
    far, near, rows, core = bit_groups()
    z_masks = [0] + far
    plane = [0] + near + rows + [a ^ b for a in near for b in rows]
    half = [p ^ z for p in plane for z in z_masks]
    return half + [m ^ core for m in half]


def spread(block):
    far, near, rows, core = bit_groups()
    mine = jnp.stack([block] + [swap(block, m) for m in far])
    cut = mine.shape[0] // 2
    by_near = [swap(mine, m) for m in near]
    by_rows = [swap(mine, m) for m in rows]
    both = []
    for a, got_a in zip(near, by_near):
        for b, got_b in zip(rows, by_rows):
            both.append(swap(got_a[:cut], b))
            both.append(swap(got_b[cut:], a))
    first = jnp.concatenate([mine] + by_near + by_rows + both)
    cut = first.shape[0] // 2
    first, second = first[:cut], first[cut:]
    return [first, second, swap(first, core), swap(second, core)]


def gather_sum(keep, send):
    far, near, rows, core = bit_groups()
    n_far, n_near, n_rows = len(far) + 1, len(near), len(rows)
    wide = jnp.float32
    cut = n_far // 2

    def add(*terms):
        return functools.reduce(jnp.add, [t.astype(wide) for t in terms]).astype(keep.dtype)

    got = swap(send, core)

    def own(i, low=0, high=n_far):
        at = slice(i * n_far + low, i * n_far + high)
        return add(keep[at], got[at])

    base = 1 + n_near + n_rows
    near_low = [own(1 + i, 0, cut) for i in range(n_near)]
    near_high = [[own(1 + i, cut)] for i in range(n_near)]
    rows_low = [[own(1 + n_near + j, 0, cut)] for j in range(n_rows)]
    rows_high = [own(1 + n_near + j, cut) for j in range(n_rows)]
    for i, a in enumerate(near):
        for j, b in enumerate(rows):
            at = base + i * n_rows + j
            rows_low[j].append(swap(own(at, 0, cut), a))
            near_high[i].append(swap(own(at, cut), b))
    low, high = [own(0, 0, cut)], [own(0, cut)]
    for i, a in enumerate(near):
        low.append(swap(near_low[i], a))
        high.append(swap(add(*near_high[i]), a))
    for j, b in enumerate(rows):
        low.append(swap(add(*rows_low[j]), b))
        high.append(swap(rows_high[j], b))
    mine = [add(*[t[i] for t in low]) for i in range(cut)]
    mine += [add(*[t[i] for t in high]) for i in range(n_far - cut)]
    total = mine[0].astype(wide)
    for m, piece in zip(far, mine[1:]):
        total = total + swap(piece, m).astype(wide)
    return total


def take_blocks_kernel(order_ref, *refs):
    column = 0
    for ref in refs[:-1]:
        width = ref.shape[-1]
        refs[-1][0, :, column : column + width] = ref[0].astype(refs[-1].dtype)
        column += width


def take_blocks(arrays, order):
    count = order.shape[0]
    blocks = [a.reshape((count, a.shape[0] // count, a.shape[1])) for a in arrays]
    rows, width = blocks[0].shape[1], sum(a.shape[1] for a in arrays)
    return pl.pallas_call(
        take_blocks_kernel,
        out_shape=jax.ShapeDtypeStruct((count, rows, width), jnp.bfloat16),
        grid_spec=pltpu.PrefetchScalarGridSpec(
            num_scalar_prefetch=1,
            grid=(count,),
            in_specs=[
                pl.BlockSpec((1, rows, a.shape[2]), lambda g, order: (order[g], 0, 0)) for a in blocks
            ],
            out_specs=pl.BlockSpec((1, rows, width), lambda g, order: (g, 0, 0)),
        ),
        name="take_blocks",
    )(order, *blocks)


def pack_kernel(fs, w_ref, u_ref):
    slices = u_ref.shape[0]
    for s in range(slices):
        for p in range(3):
            u_ref[s, :, p * fs : (p + 1) * fs] = w_ref[0, :, (p * slices + s) * fs : (p * slices + s + 1) * fs]


def pack_units(weight, slices):
    local, dl, cols = weight.shape
    fs = cols // 3 // slices
    return pl.pallas_call(
        functools.partial(pack_kernel, fs),
        out_shape=jax.ShapeDtypeStruct((local * slices, dl, 3 * fs), weight.dtype),
        grid=(local,),
        in_specs=[pl.BlockSpec((1, dl, cols), lambda g: (g, 0, 0))],
        out_specs=pl.BlockSpec((slices, dl, 3 * fs), lambda g: (g, 0, 0)),
        name="pack_units",
    )(weight)


def unpack_kernel(fs, u_ref, w_ref):
    slices = u_ref.shape[0]
    for s in range(slices):
        for p in range(3):
            w_ref[0, :, (p * slices + s) * fs : (p * slices + s + 1) * fs] = u_ref[
                s, :, p * fs : (p + 1) * fs
            ].astype(w_ref.dtype)


def unpack_units(units, slices):
    count, dl, width = units.shape
    fs, local = width // 3, count // slices
    return pl.pallas_call(
        functools.partial(unpack_kernel, fs),
        out_shape=jax.ShapeDtypeStruct((local, dl, width * slices), jnp.float32),
        grid=(local,),
        in_specs=[pl.BlockSpec((slices, dl, width), lambda g: (g, 0, 0))],
        out_specs=pl.BlockSpec((1, dl, width * slices), lambda g: (g, 0, 0)),
        name="unpack_units",
    )(units)


def unit_plan(local_count, fsdp_count):
    slices = fsdp_count // math.gcd(local_count, fsdp_count)
    per = local_count * slices // fsdp_count
    table = []
    for place in range(fsdp_count):
        owners = [(per * place + i) // slices for i in range(per)]
        second = owners[-1] if owners[-1] != owners[0] else -1
        table.append([owners[0], second] + [o - owners[0] for o in owners])
    return slices, per, np.array(table, np.int32)


def moe_kernel(per, sel_ref, x0, x1, x2, x3, c0, c1, c2, c3, routes_ref, router_ref, w_ref,
               y_keep, y_send, dx_keep, dx_send, dg_ref, dw_ref,
               x_buf, c_buf, rows_x, rows_c, dboth_s, gh_s, hot_s, gate_s, y_acc, dx_acc, dgs_s, sems, *dw_acc):
    step = pl.program_id(0)
    steps = 4 * x0.shape[0] // x_buf.shape[1]
    _, sb, length, width = x_buf.shape
    each = steps // 4

    def fetch(k):
        at = pl.ds((k % each) * sb, sb)
        for n, (pieces, buf) in enumerate((((x0, x1, x2, x3), x_buf), ((c0, c1, c2, c3), c_buf))):
            pltpu.make_async_copy(pieces[k // each].at[at], buf.at[k % 2], sems.at[n, k % 2]).start()

    @pl.when(step == 0)
    def _():
        fetch(0)

    for k in range(1, steps):

        @pl.when(step == k - 1)
        def _():
            fetch(k)

    slot = lax.rem(step, 2)
    for n, buf in enumerate((x_buf, c_buf)):
        pltpu.make_async_copy(x0.at[pl.ds(0, sb)], buf.at[slot], sems.at[n, slot]).wait()
    x_ref, cot_ref = x_buf.at[slot], c_buf.at[slot]
    fs = w_ref.shape[-1] // 3
    rows = sb * CAP
    f32, bf16 = jnp.float32, jnp.bfloat16
    experts = router_ref.shape[0]
    first, second = sel_ref[0], sel_ref[1]
    round_steps = rows_x.shape[1] // rows
    base = lax.rem(step, round_steps) * rows
    lane = lax.broadcasted_iota(jnp.int32, (length, length), 1)
    sub = lax.broadcasted_iota(jnp.int32, (length, length), 0)
    before = jnp.where(sub < lane, 1.0, 0.0).astype(bf16)
    slot_iota = lax.broadcasted_iota(jnp.int32, (CAP, length), 0)
    expert_iota = lax.broadcasted_iota(jnp.int32, (experts, length), 0)
    masks = []
    for s in range(sb):
        r = routes_ref[s]
        for e in (first, second):
            masks.append(jnp.sum(jnp.where(r == e, 1.0, 0.0), axis=0, keepdims=True))
    mask_all = jnp.concatenate(masks, axis=0)
    slot_all = jnp.dot(mask_all.astype(bf16), before, preferred_element_type=f32).astype(jnp.int32)
    for s in range(sb):
        r = routes_ref[s]
        x = x_ref[s]
        c = cot_ref[s]
        logits = lax.dot_general(router_ref[...], x, (((1,), (1,)), ((), ())), preferred_element_type=f32)
        chosen = jnp.zeros((experts, length), f32)
        for j in range(r.shape[0]):
            chosen = chosen + jnp.where(r[j : j + 1, :] == expert_iota, 1.0, 0.0)
        expo = jnp.where(chosen > 0.0, jnp.exp(logits), 0.0)
        gates = expo / jnp.sum(expo, axis=0, keepdims=True)
        hots = []
        for k, e in enumerate((first, second)):
            row = 2 * s + k
            hot = jnp.where(
                (slot_iota == slot_all[row : row + 1, :]) & (mask_all[row : row + 1, :] > 0.0), 1.0, 0.0
            )
            grow = jnp.sum(jnp.where(expert_iota == e, gates, 0.0), axis=0, keepdims=True)
            gate_s[k, pl.ds(s * CAP, CAP), :] = jnp.sum(hot * grow, axis=1, keepdims=True)
            hots.append(hot)
        hot2 = jnp.concatenate(hots, axis=0).astype(bf16)
        hot_s[s] = hot2
        got_x = jnp.dot(hot2, x, preferred_element_type=f32).astype(bf16)
        got_c = jnp.dot(hot2, c, preferred_element_type=f32).astype(bf16)
        for k in range(2):
            at = pl.ds(pl.multiple_of(base + s * CAP, CAP), CAP)
            rows_x[k, at, :] = got_x[k * CAP : (k + 1) * CAP]
            rows_c[k, at, :] = got_c[k * CAP : (k + 1) * CAP]
    y_acc[...] = jnp.zeros_like(y_acc)
    dx_acc[...] = jnp.zeros_like(dx_acc)
    dgs_s[...] = jnp.zeros_like(dgs_s)
    here = pl.ds(pl.multiple_of(base, rows), rows)
    for i in range(per):
        k = sel_ref[2 + i]
        w = w_ref[:, i].reshape(width, 3 * fs)
        w_gu, w_d = w[:, : 2 * fs], w[:, 2 * fs :]
        both = jnp.dot(rows_x[k, here, :], w_gu, preferred_element_type=f32)
        gate, up = both[:, :fs], both[:, fs:]
        sig = jax.nn.sigmoid(gate)
        hidden = (gate * sig * up).astype(bf16).astype(f32)
        dh_raw = jnp.dot(rows_c[k, here, :], w_d, preferred_element_type=f32)
        g = gate_s[k]
        dgs_s[k] += jnp.sum(hidden * dh_raw, axis=1, keepdims=True)
        dh = g * dh_raw
        dboth = jnp.concatenate(
            [dh * up * sig * (1.0 + gate * (1.0 - sig)), dh * gate * sig], axis=1
        ).astype(bf16)
        gh = (g * hidden).astype(bf16)
        dboth_s[i, here, :] = dboth
        gh_s[i, here, :] = gh
        contract = (((1,), (1,)), ((), ()))
        y_acc[k] += lax.dot_general(gh, w_d, contract, preferred_element_type=f32)
        dx_acc[k] += lax.dot_general(dboth, w_gu, contract, preferred_element_type=f32)
    contract = (((0,), (0,)), ((), ()))
    for s in range(sb):
        at = pl.ds(s * CAP, CAP)
        hot2 = hot_s[s]
        y2 = jnp.concatenate([y_acc[0, at, :], y_acc[1, at, :]], axis=0).astype(bf16)
        y = lax.dot_general(hot2, y2, contract, preferred_element_type=f32).astype(bf16)
        d2 = jnp.concatenate([dx_acc[0, at, :], dx_acc[1, at, :]], axis=0).astype(bf16)
        d = lax.dot_general(hot2, d2, contract, preferred_element_type=f32).astype(bf16)

        @pl.when(step < steps // 2)
        def _():
            y_keep[s] = y
            dx_keep[s] = d

        @pl.when(step >= steps // 2)
        def _():
            y_send[s] = y
            dx_send[s] = d

        hot = hot2.astype(f32)
        for k in range(2):
            dg_ref[s, k : k + 1, :] = jnp.sum(
                hot[k * CAP : (k + 1) * CAP] * dgs_s[k, at, :], axis=0, keepdims=True
            )

    @pl.when(lax.rem(step, round_steps) == round_steps - 1)
    def _():
        places, _, dl, _ = dw_ref.shape
        for i in range(per):
            k = sel_ref[2 + i]
            gu = lax.dot_general(rows_x[k], dboth_s[i], contract, preferred_element_type=f32)
            dd = lax.dot_general(rows_c[k], gh_s[i], contract, preferred_element_type=f32)
            if dw_acc:
                gu = gu + jnp.where(step < round_steps, 0.0, dw_acc[0][i, :, : 2 * fs])
                dd = dd + jnp.where(step < round_steps, 0.0, dw_acc[0][i, :, 2 * fs :])
                dw_acc[0][i, :, : 2 * fs] = gu
                dw_acc[0][i, :, 2 * fs :] = dd
            dw_ref[:, i, :, : 2 * fs] = gu.astype(bf16).reshape(places, dl, 2 * fs)
            dw_ref[:, i, :, 2 * fs :] = dd.astype(bf16).reshape(places, dl, fs)


def moe(sel, x_pieces, cot_pieces, routes_all, router_t, units):
    quarter, length, width = x_pieces[0].shape
    count = 4 * quarter
    places, per, dl, cols = units.shape
    fs = cols // 3
    sb = 4
    steps = count // sb
    half = steps // 2
    bf16, f32 = jnp.bfloat16, jnp.float32
    rounds = max(1, count // 32)
    slots = count * CAP // rounds
    keep = pl.BlockSpec((sb, length, width), lambda g, sel: (jnp.minimum(g, half - 1), 0, 0))
    send = pl.BlockSpec((sb, length, width), lambda g, sel: (jnp.maximum(g - half, 0), 0, 0))
    part = jax.ShapeDtypeStruct((2 * quarter, length, width), bf16)
    whole4 = lambda g, sel: (0, 0, 0, 0)
    return pl.pallas_call(
        functools.partial(moe_kernel, per),
        out_shape=(
            part,
            part,
            part,
            part,
            jax.ShapeDtypeStruct((count, 2, length), f32),
            jax.ShapeDtypeStruct(units.shape, bf16),
        ),
        grid_spec=pltpu.PrefetchScalarGridSpec(
            num_scalar_prefetch=1,
            grid=(steps,),
            in_specs=[pl.BlockSpec(memory_space=pl.ANY)] * 8
            + [
                pl.BlockSpec((sb,) + routes_all.shape[1:], lambda g, sel: (g, 0, 0)),
                pl.BlockSpec(router_t.shape, lambda g, sel: (0, 0), pipeline_mode=pl.Buffered(1)),
                pl.BlockSpec(units.shape, whole4, pipeline_mode=pl.Buffered(1)),
            ],
            out_specs=[
                keep,
                send,
                keep,
                send,
                pl.BlockSpec((sb, 2, length), lambda g, sel: (g, 0, 0)),
                pl.BlockSpec(units.shape, whole4, pipeline_mode=pl.Buffered(1)),
            ],
            scratch_shapes=[
                pltpu.VMEM((2, sb, length, width), bf16),
                pltpu.VMEM((2, sb, length, width), bf16),
                pltpu.VMEM((2, slots, width), bf16),
                pltpu.VMEM((2, slots, width), bf16),
                pltpu.VMEM((per, slots, 2 * fs), bf16),
                pltpu.VMEM((per, slots, fs), bf16),
                pltpu.VMEM((sb, 2 * CAP, length), bf16),
                pltpu.VMEM((2, sb * CAP, 1), f32),
                pltpu.VMEM((2, sb * CAP, width), f32),
                pltpu.VMEM((2, sb * CAP, width), f32),
                pltpu.VMEM((2, sb * CAP, 1), f32),
                pltpu.SemaphoreType.DMA((2, 2)),
            ]
            + [pltpu.VMEM((per, width, cols), f32)] * (rounds > 1),
        ),
        compiler_params=pltpu.CompilerParams(
            dimension_semantics=("arbitrary",), vmem_limit_bytes=60 << 20
        ),
        cost_estimate=pl.CostEstimate(
            flops=2 * count * CAP * per * fs * width * 9,
            transcendentals=count * CAP * per * fs,
            bytes_accessed=4 * count * length * width * 2,
        ),
        name="moe",
    )(sel, *x_pieces, *cot_pieces, routes_all, router_t, units)


def on_device(
    tokens,
    seq_ids,
    routes,
    cotangent,
    gain_attn,
    qkv_weight,
    out_weight,
    gain_moe,
    router_weight,
    expert_weight,
):
    length = tokens.shape[0]
    fsdp_count = lax.axis_size("fsdp")
    dp_count = lax.axis_size("dp")
    count = dp_count * fsdp_count
    local_count, dl, cols = expert_weight.shape
    hidden_width = cols // 3
    slices, per, table = unit_plan(local_count, fsdp_count)
    fs = hidden_width // slices
    query_width = H * HD
    kv_width = KV * HD
    group_size = H // KV
    factor = HD ** (-0.5)
    bf16, f32 = jnp.bfloat16, jnp.float32
    dp_at, fsdp_at = lax.axis_index("dp"), lax.axis_index("fsdp")
    me = dp_at * fsdp_count + fsdp_at
    order = jnp.asarray(np.array(mask_order(), np.int32)) ^ me

    own_rows = qkv_weight.shape[0]
    route_cols = -(-routes.size // own_rows)
    coded = jnp.zeros((own_rows * route_cols,), bf16).at[: routes.size].set(routes.T.reshape(-1).astype(bf16))
    coded = coded.reshape(own_rows, route_cols)
    pad = jnp.zeros((own_rows, 128 - E - 2 - route_cols), bf16)
    small = jnp.concatenate(
        [qkv_weight, router_weight, gain_attn[:, None], gain_moe[:, None], coded, pad], axis=1
    )
    qkv_small = lax.all_gather(small, AXES, axis=0, tiled=True)
    out_full = lax.all_gather(out_weight, AXES, axis=0, tiled=True)
    qkv_full = qkv_small[:, : qkv_weight.shape[1]]
    tail = qkv_small[:, qkv_weight.shape[1] :]
    router_full, gain_one, gain_two = tail[:, :E], tail[:, E], tail[:, E + 1]
    routes_all = tail.reshape(count, own_rows, 128)[:, :, E + 2 : E + 2 + route_cols].reshape(count, -1)
    routes_all = routes_all[:, : routes.size].reshape(count, routes.shape[1], length).astype(jnp.int32)
    routes_all = routes_all[order]

    units = pack_units(expert_weight, slices).reshape(fsdp_count, per, dl, 3 * fs)
    units = lax.all_to_all(units, "fsdp", split_axis=0, concat_axis=0, tiled=True)
    cot_all = spread(cotangent)
    sel = jnp.asarray(table)[fsdp_at]
    shift = jnp.where(sel[:2] >= 0, dp_at * local_count, 0)
    sel = jnp.concatenate([sel[:2] + shift, sel[2:]])

    cosine, sine_table, visible = rope_tables(seq_ids[0], HD // 2)
    stream_in = tokens.astype(f32)
    inv_one, normed = norm_forward(stream_in, gain_one)
    normed_one = normed.astype(bf16)
    qkv_proj = jnp.dot(normed_one, qkv_full, preferred_element_type=f32)
    queries = rotate(qkv_proj[:, :query_width].reshape(length, H, HD), cosine, sine_table).astype(bf16)
    keys_rot = rotate(
        qkv_proj[:, query_width : query_width + kv_width].reshape(length, KV, HD), cosine, sine_table
    ).astype(bf16)
    values_in = qkv_proj[:, query_width + kv_width :].reshape(length, KV, HD).astype(bf16)
    query_groups = queries.reshape(length, KV, group_size, HD).transpose(1, 2, 0, 3)
    key_groups = keys_rot.transpose(1, 0, 2)
    value_groups = values_in.transpose(1, 0, 2)

    def forward_group(group_in):
        return attend_group(group_in, visible, factor)

    mixed_groups, log_totals = lax.map(forward_group, (query_groups, key_groups, value_groups))
    mixed_flat = mixed_groups.transpose(2, 0, 1, 3).reshape(length, query_width)
    resid_mid = stream_in + jnp.dot(mixed_flat, out_full, preferred_element_type=f32)
    inv_two, normed = norm_forward(resid_mid, gain_two)
    normed_two = normed.astype(bf16)

    x_all = spread(normed_two)
    y_keep, y_send, dx_keep, dx_send, dg_parts, dw_units = moe(sel, x_all, cot_all, routes_all, router_full.T, units)

    logits = jnp.dot(normed_two, router_full, preferred_element_type=f32)
    chosen = jnp.any(routes[:, :, None] == jnp.arange(E)[None, None, :], axis=1)
    expo = jnp.where(chosen, jnp.exp(logits), 0.0)
    gates = expo / jnp.sum(expo, axis=-1, keepdims=True)
    inverse = jnp.asarray(np.argsort(np.array(mask_order())).astype(np.int32))
    dg_natural = dg_parts[inverse[jnp.arange(count) ^ me]]
    dg_got = lax.all_to_all(dg_natural, AXES, split_axis=0, concat_axis=0, tiled=True)
    owner = np.zeros((E, count, 2), np.float32)
    for device in range(count):
        for k in range(2):
            local = table[device % fsdp_count, k]
            if local >= 0:
                owner[(device // fsdp_count) * local_count + local, device, k] = 1.0
    d_gates = jnp.einsum("edk,dkt->te", jnp.asarray(owner), dg_got, precision=lax.Precision.HIGHEST)
    d_gates = jnp.where(chosen, d_gates, 0.0)
    d_logits = (gates * (d_gates - jnp.sum(gates * d_gates, axis=-1, keepdims=True))).astype(bf16)

    d_normed_two = gather_sum(dx_keep, dx_send) + jnp.dot(d_logits, router_full.T, preferred_element_type=f32)
    d_block = cotangent.astype(f32)
    d_router = jnp.dot(normed_two.T, d_logits, preferred_element_type=f32)
    d_resid, d_gain_two = norm_backward(resid_mid, inv_two, gain_two, d_normed_two)
    d_resid = d_resid + d_block
    d_resid_half = d_resid.astype(bf16)
    d_out = jnp.dot(mixed_flat.T, d_resid_half, preferred_element_type=f32)
    d_mixed = jnp.dot(d_resid_half, out_full.T, preferred_element_type=f32).astype(bf16)
    d_mixed_groups = d_mixed.reshape(length, KV, group_size, HD).transpose(1, 2, 0, 3)

    def backward_group(group_in):
        return attend_back(group_in, visible, factor)

    d_query, d_keys, d_values = lax.map(
        backward_group,
        (query_groups, key_groups, value_groups, mixed_groups, log_totals, d_mixed_groups),
    )
    d_query = unrotate(d_query.transpose(2, 0, 1, 3).reshape(length, H, HD), cosine, sine_table)
    d_keys = unrotate(d_keys.transpose(1, 0, 2), cosine, sine_table)
    d_qkv_act = jnp.concatenate(
        [
            d_query.reshape(length, query_width),
            d_keys.reshape(length, kv_width),
            d_values.transpose(1, 0, 2).reshape(length, kv_width),
        ],
        axis=-1,
    ).astype(bf16)
    d_qkv = jnp.dot(normed_one.T, d_qkv_act, preferred_element_type=f32)
    d_normed_one = jnp.dot(d_qkv_act, qkv_full.T, preferred_element_type=f32)
    d_stream, d_gain_one = norm_backward(stream_in, inv_one, gain_one, d_normed_one)
    d_tokens = d_stream + d_resid

    block_out = (resid_mid + gather_sum(y_keep, y_send)).astype(bf16)
    d_out = take_blocks([d_out], order)
    d_out_weight = gather_sum(d_out[: count // 2], d_out[count // 2 :])
    thin = jnp.concatenate(
        [d_router, d_gain_one[:, None], d_gain_two[:, None], jnp.zeros((D, 128 - E - 2), f32)], axis=1
    )
    d_qkv = take_blocks([d_qkv, thin], order)
    d_qkv = gather_sum(d_qkv[: count // 2], d_qkv[count // 2 :])
    d_qkv_weight, thin = d_qkv[:, : qkv_weight.shape[1]], d_qkv[:, qkv_weight.shape[1] :]
    dw = lax.all_to_all(dw_units, "fsdp", split_axis=0, concat_axis=0, tiled=True)
    d_expert_weight = unpack_units(dw.reshape(local_count * slices, dl, 3 * fs), slices)
    return (
        block_out,
        d_tokens,
        thin[:, E],
        d_qkv_weight,
        d_out_weight,
        thin[:, E + 1],
        thin[:, :E],
        d_expert_weight,
    )


def solution(mesh):
    rows = P(AXES, None)
    in_specs = (rows, rows, rows, rows, P(AXES), rows, rows, P(AXES), rows, P("dp", "fsdp", None))
    out_specs = (rows, rows, P(AXES), rows, rows, P(AXES), rows, P("dp", "fsdp", None))
    return jax.shard_map(
        on_device, mesh=mesh, in_specs=in_specs, out_specs=out_specs, check_vma=False
    )
```
